256 devices in a mesh: seq: 32 (over z, y_hi, core), chan: 8 (over y_lo, x).
Axes of the slice: x: 4, y: 4 (y_hi: 2, y_lo: 2; y = y_hi * 2 + y_lo), z: 8, core: 2. Of those that a mesh axis runs over, the one named last changes fastest.
Arguments:
- tokens: bfloat16 [384, 512, 1024], P('chan', 'seq'), may hold values from -6 to 6
- gating: bfloat16 [384, 512, 1024], P(None, ('seq', 'chan')), may hold values from -6 to 6
- kernel: bfloat16 [384, 1024, 512], P('chan', 'seq'), may hold values from -6 to 6
- first_factor: bfloat16 [1024, 1024], replicated, may hold values from -0.1875 to 0.1875
- first_twiddle: float32 [512, 1024], P('seq'), may hold values from 0.5 to 1.5
- second_factor: bfloat16 [512, 512], replicated, may hold values from -0.25 to 0.25
- inverse_second: bfloat16 [512, 512], replicated, may hold values from -0.25 to 0.25
- inverse_twiddle: float32 [1024, 512], P('seq'), may hold values from 0.5 to 1.5
- inverse_first: bfloat16 [1024, 1024], replicated, may hold values from -0.1875 to 0.1875
- projection: bfloat16 [384, 384], replicated, may hold values from -0.3125 to 0.3125
Outputs:
- result: bfloat16 [384, 512, 1024], P(None, ('seq', 'chan'))
The draws below stay inside these ranges and needn't reach their ends.
All inputs are finite; a program needn't handle non-finite values.
Results may differ from the reference program's by a relative error of at most 0.012.
Values may be sent and summed in bfloat16 or wider, within the bound.
A program may use at most 64 MiB of HBM per device.

```python
from functools import partial
import jax
import jax.numpy as jnp
from jax import lax

D = 384
A = 512
B = 1024


def block_levels(key, shape, split, smallest, top_value):
    factor_of, own = 1.0, jax.random.fold_in(key, 6)
    for axis_at, blocks in split:
        steps = jnp.exp(jax.random.uniform(jax.random.fold_in(own, axis_at), (blocks,), jnp.float32, smallest / len(split), top_value / len(split)))
        factor_of = factor_of * jnp.repeat(steps, shape[axis_at] // blocks).reshape([-1 if axis == axis_at else 1 for axis in range(len(shape))])
    return factor_of


def bell_draw(stream_key, shape, width, limit, pieces=(), kind=jnp.bfloat16):
    factor_of = block_levels(stream_key, shape, pieces, -0.22, 0.18) if pieces else 1.0
    values = jax.random.normal(stream_key, shape, jnp.float32) * width * factor_of
    return jnp.minimum(jnp.maximum(values, -limit), limit).astype(kind)


def setup_inputs(seed: int = 0) -> dict:
    streams_of = jax.random.split(jax.random.key(seed), 11)
    tokens = bell_draw(streams_of[0], (D, A, B), 1.0, 6.0, ((0, 8), (1, 32)))
    gating = bell_draw(streams_of[1], (D, A, B), 1.0, 6.0, ((1, 256),))
    kernel = bell_draw(streams_of[2], (D, B, A), 1.0, 6.0, ((0, 8), (1, 32)))
    first_factor = bell_draw(streams_of[3], (B, B), B ** -0.5, 0.1875)
    first_twiddle = jnp.clip(0.5 + 1.0 * jax.random.uniform(streams_of[4], (A, B), jnp.float32) ** block_levels(streams_of[4], (A, B), ((0, 32),), -0.2, 0.2), 0.5, 1.5)
    second_factor = bell_draw(streams_of[5], (A, A), A ** -0.5, 0.25)
    inverse_second = bell_draw(streams_of[6], (A, A), A ** -0.5, 0.25)
    inverse_twiddle = jnp.clip(0.5 + 1.0 * jax.random.uniform(streams_of[7], (B, A), jnp.float32) ** block_levels(streams_of[7], (B, A), ((0, 32),), -0.2, 0.2), 0.5, 1.5)
    inverse_first = bell_draw(streams_of[8], (B, B), B ** -0.5, 0.1875)
    projection = bell_draw(streams_of[9], (D, D), D ** -0.5, 0.3125)
    return dict(tokens=tokens, gating=gating, kernel=kernel, first_factor=first_factor, first_twiddle=first_twiddle, second_factor=second_factor, inverse_second=inverse_second, inverse_twiddle=inverse_twiddle, inverse_first=inverse_first, projection=projection)


def channel_mix(operands, first_factor, first_twiddle, second_factor, inverse_second, inverse_twiddle, inverse_first):
    signal, spectral, gate_plane = operands
    first = (jnp.dot(signal, first_factor.T, preferred_element_type=jnp.float32) * first_twiddle).astype(jnp.bfloat16)
    spectrum = jnp.dot(first.T, second_factor.T, preferred_element_type=jnp.float32)
    scaled = (spectrum * spectral.astype(jnp.float32)).astype(jnp.bfloat16)
    inverse = (jnp.dot(scaled, inverse_second.T, preferred_element_type=jnp.float32) * inverse_twiddle).astype(jnp.bfloat16)
    mixed = jnp.dot(inverse.T, inverse_first.T, preferred_element_type=jnp.float32).astype(jnp.bfloat16)
    return (mixed.astype(jnp.float32) * gate_plane.astype(jnp.float32)).astype(jnp.bfloat16)


def reference(tokens, gating, kernel, first_factor, first_twiddle, second_factor, inverse_second, inverse_twiddle, inverse_first, projection):
    mixer = partial(channel_mix, first_factor=first_factor, first_twiddle=first_twiddle, second_factor=second_factor, inverse_second=inverse_second, inverse_twiddle=inverse_twiddle, inverse_first=inverse_first)
    gated = lax.map(mixer, (tokens, kernel, gating))

    def project(rows):
        return jnp.dot(projection.T, rows, preferred_element_type=jnp.float32).astype(jnp.bfloat16)

    result = lax.map(project, jnp.swapaxes(gated, 0, 1))
    return jnp.swapaxes(result, 0, 1)
```

```python
import functools

import jax
import jax.numpy as jnp
from jax import lax
from jax.experimental import pallas as pl
from jax.experimental.pallas import tpu as pltpu
from jax.sharding import PartitionSpec as P

MESH = pl.DeviceIdType.MESH
F32 = jnp.float32
BF16 = jnp.bfloat16
SEQ, CHAN = 32, 8
CL, AL, B, A, KL, D = 48, 16, 1024, 512, 32, 384
CH = 16
NH = CL // CH
WH = CH * KL
CQ = 8
NQ = CL // CQ
W = CQ * KL
FAR = [d for k in range(17) for d in sorted({16 - k, 16 + k}) if 0 < d < SEQ]


def nt(a, b):
    return lax.dot_general(a, b, (((1,), (1,)), ((), ())), preferred_element_type=F32)


def swap_groups(v, hi, odd):
    v0, v1, v2, v3 = v
    a0 = jnp.where(hi, pltpu.roll(v2, 64, 1), v0)
    a2 = jnp.where(hi, v2, pltpu.roll(v0, 64, 1))
    a1 = jnp.where(hi, pltpu.roll(v3, 64, 1), v1)
    a3 = jnp.where(hi, v3, pltpu.roll(v1, 64, 1))
    o0 = jnp.where(odd, pltpu.roll(a1, 32, 1), a0)
    o1 = jnp.where(odd, a1, pltpu.roll(a0, 96, 1))
    o2 = jnp.where(odd, pltpu.roll(a3, 32, 1), a2)
    o3 = jnp.where(odd, a3, pltpu.roll(a2, 96, 1))
    return o0, o1, o2, o3


def at(i, n):
    return pl.ds(pl.multiple_of(i * n, n), n)


def mixer(
    tok_h, gat_h, ker_h, f1_h, tw1_h, s2_h, v2_h, tw2_h, u1_h, pr_h,
    gd, pt,
    tok, gat, ker, f1, tw1, s2, v2, tw2, u1, pr,
    snd1, xin, cnd, cin, snd2, zin, kt_, tw2t, v2p, tw2p, gp, lb, sf, sp,
    fsem, tsem, lsem, ssem, xsem, csem, zsem,
):
    me = lax.axis_index("seq")
    mc = lax.axis_index("chan")
    n0 = lax.rem(lax.div(me, 8) + 2, 4)

    def f1_load(i):
        rows = at(lax.rem(n0 + i, 4), 256)
        return pltpu.make_async_copy(f1_h.at[rows], f1.at[rows], fsem.at[i])

    def tok_load(h):
        rows = pl.ds(h * CH, CH)
        return pltpu.make_async_copy(tok_h.at[rows], tok.at[rows], tsem.at[h])

    loads = [
        pltpu.make_async_copy(src, dst, lsem.at[i])
        for i, (src, dst) in enumerate(
            [(tw1_h, tw1), (s2_h, s2), (ker_h, ker), (v2_h, v2), (tw2_h, tw2), (u1_h, u1), (pr_h, pr)]
            + [(gat_h.at[pl.ds(p * CL, CL)], gat.at[:, p]) for p in range(CHAN)]
        )
    ]
    tok_load(0).start()
    f1_load(0).start()
    loads[0].start()

    barrier = pltpu.get_barrier_semaphore()
    for d in FAR:
        pl.semaphore_signal(barrier, inc=1, device_id={"seq": lax.rem(me + d, SEQ)}, device_id_type=MESH)
    for d in range(1, CHAN):
        pl.semaphore_signal(barrier, inc=1, device_id={"chan": lax.rem(mc + d, CHAN)}, device_id_type=MESH)

    for i in range(1, 4):
        f1_load(i).start()
    for h in range(1, NH):
        tok_load(h).start()
    for c in loads[1:]:
        c.start()

    lane = lax.broadcasted_iota(jnp.int32, (16, 128), 1)
    hi = lane >= 64
    odd = lax.rem(lax.div(lane, 32), 2) == 1

    def send(src, dst, sem, p, lanes):
        pltpu.make_async_remote_copy(
            src.at[p, :, lanes], dst.at[me, :, lanes], ssem.at[0], sem,
            device_id={"seq": p}, device_id_type=MESH,
        ).start()

    def arrived(dst, sem, lanes):
        block = dst.at[pl.ds(0, SEQ - 1), :, lanes]
        pltpu.make_async_copy(block, block, sem).wait()

    loads[0].wait()
    for h in range(NH):
        tok_load(h).wait()
        lanes = pl.ds(h * WH, WH)

        def first(i, c, h=h, lanes=lanes):
            n = lax.rem(n0 + i, 4)
            if h == 0:
                f1_load(i).wait()
            rows = tok[pl.ds(h * CH, CH)].reshape(CH * AL, B)
            f = nt(rows, f1[at(n, 256), :])
            for t in range(2):
                tw = tw1[:, at(2 * n + t, 128)]
                for g in range(CH // 4):
                    tiles = [f[(4 * g + j) * 16:(4 * g + j + 1) * 16, t * 128:(t + 1) * 128] * tw for j in range(4)]
                    outs = swap_groups(tiles, hi, odd)
                    for j in range(4):
                        snd1[n * 8 + t * 4 + j, :, h * WH + g * 128:h * WH + (g + 1) * 128] = outs[j].astype(BF16)
            if h == 0:
                @pl.when(i == 0)
                def _():
                    pl.semaphore_wait(barrier, SEQ - 1 + CHAN - 1)
            for j in range(8):
                p = n * 8 + j

                @pl.when(p != me)
                def _(p=p):
                    send(snd1, xin, xsem.at[h], p, lanes)

            return c

        lax.fori_loop(0, 4, first, 0)
        xin[me, :, lanes] = snd1[me, :, lanes]

    for c in loads[1:]:
        c.wait()

    def flip(q, c):
        k = ker[pl.ds(q * CQ, CQ)].reshape(W, A)
        kt_[q] = k.T
        return c

    lax.fori_loop(0, NQ, flip, 0)
    t = tw2[...]
    tw2t[...] = jnp.concatenate([t, t, t, t], axis=0).T
    for k in range(A // 128):
        sf[...] = v2[:, k * 128:(k + 1) * 128].astype(F32)

        def order(i, c, k=k):
            v2p[at(i, SEQ), k * 128:(k + 1) * 128] = sf[pl.ds(i, SEQ, stride=16), :].astype(BF16)
            if k == 0:
                tw2p[at(i, SEQ), :] = tw2t[pl.ds(i, SEQ, stride=16), :]
            return c

        lax.fori_loop(0, 16, order, 0)

    def middle(q):
        lanes = at(q, W)
        x = xin[:, :, lanes].reshape(A, W)
        spectrum = jnp.dot(s2[...], x, preferred_element_type=F32)
        scaled = (spectrum * kt_[q].astype(F32)).astype(BF16)
        inv = jnp.dot(v2p[...], scaled, preferred_element_type=F32)
        tw = tw2p[...]
        inv = (inv * jnp.concatenate([tw] * (W // 128), axis=1)).astype(BF16)
        cnd[q] = inv.reshape(CHAN, 64, W)
        cin[q, mc] = cnd[q, mc]
        for d in (4, 1, 5, 7, 3, 2, 6):
            p = lax.rem(mc + d, CHAN)
            pltpu.make_async_remote_copy(
                cnd.at[q, p], cin.at[q, mc], ssem.at[1], csem.at[q],
                device_id={"chan": p}, device_id_type=MESH,
            ).start()

    def onward(q):
        block = cin.at[q, pl.ds(0, CHAN - 1)]
        pltpu.make_async_copy(block, block, csem.at[q]).wait()
        for t in range(W // 128):
            cols = slice(t * 128, (t + 1) * 128)
            for r in range(2):
                for p in range(CHAN):
                    sf[(r * 8 + p) * 32:(r * 8 + p + 1) * 32, :] = cin[q, p, r * 32:(r + 1) * 32, cols].astype(F32)

            def pick(s, c, t=t):
                snd2[s, :, at(q * (W // 128) + t, 128)] = sf[pl.ds(s, 16, stride=SEQ), :].astype(BF16)
                return c

            lax.fori_loop(0, SEQ, pick, 0, unroll=8)
        lanes = at(q, W)
        zin[me, :, lanes] = snd2[me, :, lanes]
        for d in FAR:
            send(snd2, zin, zsem.at[q], lax.rem(me + d, SEQ), lanes)

    def stage(q, c):
        @pl.when(lax.rem(q, 2) == 0)
        def _():
            h = lax.div(q, 2)
            arrived(xin, xsem.at[h], at(h, WH))

        middle(q)

        @pl.when(q > 0)
        def _():
            onward(q - 1)

        return c

    lax.fori_loop(0, NQ, stage, 0)
    onward(NQ - 1)

    def gate_rows(i, c):
        g = gat[i].astype(F32)
        gp[at(i, 16), :] = jnp.concatenate([g[:, 0, :], g[:, 1, :]], axis=0).astype(BF16)
        return c

    lax.fori_loop(0, CL, gate_rows, 0)
    for k in range(D // 128):
        for p in range(CHAN):
            sp[pl.ds(p, CL, stride=CHAN), :] = pr[p * CL:(p + 1) * CL, k * 128:(k + 1) * 128].astype(F32)
        pt[k * 128:(k + 1) * 128, :] = sp[...].T.astype(BF16)

    def mix(q, c):
        arrived(zin, zsem.at[q], at(q, W))

        def regroup(k, c):
            for g in range(CQ // 4):
                lanes = at(q * (CQ // 4) + g, 128)
                tiles = [zin[4 * k + j, :, lanes].astype(F32) for j in range(4)]
                outs = swap_groups(tiles, hi, odd)
                for j in range(4):
                    lb[(4 * g + j) * 16:(4 * g + j + 1) * 16, at(k, 128)] = outs[j].astype(BF16)
            return c

        lax.fori_loop(0, B // 128, regroup, 0)

        def columns(n, c):
            cols = at(n, 256)
            m = nt(lb[...], u1[cols, :]).astype(BF16).astype(F32)
            m = m * gp[at(q, CQ * 16), cols].astype(F32)
            m = m.reshape(CQ, 2, CHAN, 256)
            for r in range(2):
                gd[r, at(q, CQ * CHAN), cols] = m[:, r].reshape(CQ * CHAN, 256).astype(BF16)
            return c

        lax.fori_loop(0, B // 256, columns, 0)
        return c

    lax.fori_loop(0, NQ, mix, 0)

    for buf in (snd1, snd2):
        block = buf.at[pl.ds(0, SEQ - 1)]
        pltpu.make_async_copy(block, block, ssem.at[0]).wait()
    block = cnd.at[:, pl.ds(0, CHAN - 1)]
    pltpu.make_async_copy(block, block, ssem.at[1]).wait()


def projector(gd, pt, out_h, res, sem):
    copies = []
    for n in range(B // 256):
        cols = slice(n * 256, (n + 1) * 256)
        for r in range(2):
            res[n, :, r, :] = jnp.dot(pt[...], gd[r, :, cols], preferred_element_type=F32).astype(BF16)
        copies.append(pltpu.make_async_copy(res.at[n], out_h.at[:, :, pl.ds(n * 256, 256)], sem.at[n]))
        copies[-1].start()
    for c in copies:
        c.wait()


def body(*args):
    hbm = pl.BlockSpec(memory_space=pltpu.HBM)
    whole = pl.BlockSpec(memory_space=pltpu.VMEM)
    vm = pltpu.VMEM
    dma = pltpu.SemaphoreType.DMA
    gd, pt = pl.pallas_call(
        mixer,
        out_shape=(jax.ShapeDtypeStruct((2, D, B), BF16), jax.ShapeDtypeStruct((D, D), BF16)),
        in_specs=[hbm] * 10,
        out_specs=(whole, whole),
        scratch_shapes=[
            vm((CL, AL, B), BF16), vm((CL, CHAN, 2, B), BF16), vm((CL, KL, A), BF16), vm((B, B), BF16),
            vm((AL, B), F32), vm((A, A), BF16), vm((A, A), BF16), vm((KL, A), F32), vm((B, B), BF16), vm((D, D), BF16),
            vm((SEQ, 16, CL * KL), BF16), vm((SEQ, 16, CL * KL), BF16),
            vm((NQ, CHAN, 64, W), BF16), vm((NQ, CHAN, 64, W), BF16),
            vm((SEQ, 16, CL * KL), BF16), vm((SEQ, 16, CL * KL), BF16),
            vm((NQ, A, W), BF16), vm((A, 128), F32), vm((A, A), BF16), vm((A, 128), F32),
            vm((CL * 16, B), BF16), vm((16 * CQ, B), BF16), vm((A, 128), F32), vm((D, 128), F32),
            dma((4,)), dma((NH,)), dma((15,)), dma((2,)), dma((NH,)), dma((NQ,)), dma((NQ,)),
        ],
        compiler_params=pltpu.CompilerParams(
            collective_id=0, has_side_effects=True, vmem_limit_bytes=VLIM * 1024 * 1024
        ),
    )(*[pltpu.with_memory_space_constraint(x, pltpu.HBM) for x in args])
    return pl.pallas_call(
        projector,
        out_shape=jax.ShapeDtypeStruct((D, 2, B), BF16),
        in_specs=[whole, whole],
        out_specs=hbm,
        scratch_shapes=[vm((B // 256, D, 2, 256), BF16), dma((B // 256,))],
        compiler_params=pltpu.CompilerParams(vmem_limit_bytes=32 * 1024 * 1024),
    )(gd, pt)


VLIM = 48


def solution(mesh):
    return jax.shard_map(
        body,
        mesh=mesh,
        in_specs=(
            P("chan", "seq", None),
            P(None, ("seq", "chan"), None),
            P("chan", "seq", None),
            P(),
            P("seq", None),
            P(),
            P(),
            P("seq", None),
            P(),
            P(),
        ),
        out_specs=P(None, ("seq", "chan"), None),
        check_vma=False,
    )
```

```python
import functools

import jax
import jax.numpy as jnp
from jax import lax
from jax.experimental import pallas as pl
from jax.experimental.pallas import tpu as pltpu
from jax.sharding import PartitionSpec as P

MESH = pl.DeviceIdType.MESH
F32 = jnp.float32
BF16 = jnp.bfloat16
SEQ, CHAN = 32, 8
CL, AL, B, A, KL, D = 48, 16, 1024, 512, 32, 384
CH = 16
NH = CL // CH
WH = CH * KL
CQ = 8
NQ = CL // CQ
W = CQ * KL
FAR = [d for k in range(17) for d in sorted({16 - k, 16 + k}) if 0 < d < SEQ]


def nt(a, b):
    return lax.dot_general(a, b, (((1,), (1,)), ((), ())), preferred_element_type=F32)


def swap_groups(v, hi, odd):
    v0, v1, v2, v3 = v
    a0 = jnp.where(hi, pltpu.roll(v2, 64, 1), v0)
    a2 = jnp.where(hi, v2, pltpu.roll(v0, 64, 1))
    a1 = jnp.where(hi, pltpu.roll(v3, 64, 1), v1)
    a3 = jnp.where(hi, v3, pltpu.roll(v1, 64, 1))
    o0 = jnp.where(odd, pltpu.roll(a1, 32, 1), a0)
    o1 = jnp.where(odd, a1, pltpu.roll(a0, 96, 1))
    o2 = jnp.where(odd, pltpu.roll(a3, 32, 1), a2)
    o3 = jnp.where(odd, a3, pltpu.roll(a2, 96, 1))
    return o0, o1, o2, o3


def at(i, n):
    return pl.ds(pl.multiple_of(i * n, n), n)


def mixer(
    tok_h, gat_h, ker_h, f1_h, tw1_h, s2_h, v2_h, tw2_h, u1_h, pr_h,
    acc, pb5, g5,
    tok, gat, ker, f1, tw1, s2, v2, tw2, u1, pr,
    snd1, xin, cnd, cin, snd2, zin, kt_, tw2t, v2p, tw2p, gp, lb, sf, sp, st, sb, pb, g4,
    fsem, tsem, lsem, ssem, xsem, csem, zsem,
):
    me = lax.axis_index("seq")
    mc = lax.axis_index("chan")
    n0 = lax.rem(lax.div(me, 8) + 2, 4)

    def f1_load(i):
        rows = at(lax.rem(n0 + i, 4), 256)
        return pltpu.make_async_copy(f1_h.at[rows], f1.at[rows], fsem.at[i])

    def tok_load(h):
        rows = pl.ds(h * CH, CH)
        return pltpu.make_async_copy(tok_h.at[rows], tok.at[rows], tsem.at[h])

    loads = [
        pltpu.make_async_copy(src, dst, lsem.at[i])
        for i, (src, dst) in enumerate(
            [(tw1_h, tw1), (s2_h, s2), (ker_h, ker), (v2_h, v2), (tw2_h, tw2), (u1_h, u1), (pr_h, pr)]
            + [(gat_h.at[pl.ds(p * CL, CL)], gat.at[:, p]) for p in range(CHAN)]
        )
    ]
    tok_load(0).start()
    f1_load(0).start()
    loads[0].start()

    barrier = pltpu.get_barrier_semaphore()
    for d in FAR:
        pl.semaphore_signal(barrier, inc=1, device_id={"seq": lax.rem(me + d, SEQ)}, device_id_type=MESH)
    for d in range(1, CHAN):
        pl.semaphore_signal(barrier, inc=1, device_id={"chan": lax.rem(mc + d, CHAN)}, device_id_type=MESH)

    for i in range(1, 4):
        f1_load(i).start()
    for h in range(1, NH):
        tok_load(h).start()
    for c in loads[1:]:
        c.start()

    lane = lax.broadcasted_iota(jnp.int32, (16, 128), 1)
    hi = lane >= 64
    odd = lax.rem(lax.div(lane, 32), 2) == 1

    def send(src, dst, sem, p, lanes):
        pltpu.make_async_remote_copy(
            src.at[p, :, lanes], dst.at[me, :, lanes], ssem.at[0], sem,
            device_id={"seq": p}, device_id_type=MESH,
        ).start()

    def arrived(dst, sem, lanes):
        block = dst.at[pl.ds(0, SEQ - 1), :, lanes]
        pltpu.make_async_copy(block, block, sem).wait()

    loads[0].wait()
    for h in range(NH):
        tok_load(h).wait()
        lanes = pl.ds(h * WH, WH)

        def first(i, c, h=h, lanes=lanes):
            n = lax.rem(n0 + i, 4)
            if h == 0:
                f1_load(i).wait()
            rows = tok[pl.ds(h * CH, CH)].reshape(CH * AL, B)
            f = nt(rows, f1[at(n, 256), :])
            for t in range(2):
                tw = tw1[:, at(2 * n + t, 128)]
                for g in range(CH // 4):
                    tiles = [f[(4 * g + j) * 16:(4 * g + j + 1) * 16, t * 128:(t + 1) * 128] * tw for j in range(4)]
                    outs = swap_groups(tiles, hi, odd)
                    for j in range(4):
                        snd1[n * 8 + t * 4 + j, :, h * WH + g * 128:h * WH + (g + 1) * 128] = outs[j].astype(BF16)
            if h == 0:
                @pl.when(i == 0)
                def _():
                    pl.semaphore_wait(barrier, SEQ - 1 + CHAN - 1)
            for j in range(8):
                p = n * 8 + j

                @pl.when(p != me)
                def _(p=p):
                    send(snd1, xin, xsem.at[h], p, lanes)

            return c

        lax.fori_loop(0, 4, first, 0)
        xin[me, :, lanes] = snd1[me, :, lanes]

    for c in loads[1:]:
        c.wait()

    def flip(q, c):
        k = ker[pl.ds(q * CQ, CQ)].reshape(W, A)
        kt_[q] = k.T
        return c

    lax.fori_loop(0, NQ, flip, 0)
    t = tw2[...]
    tw2t[...] = jnp.concatenate([t, t, t, t], axis=0).T
    for k in range(A // 128):
        sf[...] = v2[:, k * 128:(k + 1) * 128].astype(F32)

        def order(i, c, k=k):
            v2p[at(i, SEQ), k * 128:(k + 1) * 128] = sf[pl.ds(i, SEQ, stride=16), :].astype(BF16)
            if k == 0:
                tw2p[at(i, SEQ), :] = tw2t[pl.ds(i, SEQ, stride=16), :]
            return c

        lax.fori_loop(0, 16, order, 0)

    def middle(q):
        lanes = at(q, W)
        x = xin[:, :, lanes].reshape(A, W)
        spectrum = jnp.dot(s2[...], x, preferred_element_type=F32)
        scaled = (spectrum * kt_[q].astype(F32)).astype(BF16)
        inv = jnp.dot(v2p[...], scaled, preferred_element_type=F32)
        tw = tw2p[...]
        inv = (inv * jnp.concatenate([tw] * (W // 128), axis=1)).astype(BF16)
        cnd[q] = inv.reshape(CHAN, 64, W)
        cin[q, mc] = cnd[q, mc]
        for d in (4, 1, 5, 7, 3, 2, 6):
            p = lax.rem(mc + d, CHAN)
            pltpu.make_async_remote_copy(
                cnd.at[q, p], cin.at[q, mc], ssem.at[1], csem.at[q],
                device_id={"chan": p}, device_id_type=MESH,
            ).start()

    r4 = lax.rem(me, 4)

    def group(q, zs):
        for zz in zs:
            for dr in range(4):
                p = zz * 4 + lax.rem(r4 + dr, 4)

                @pl.when(p != me)
                def _(p=p):
                    send(snd2, zin, zsem.at[q], p, at(q, W))

    def far(q):
        for d in FAR:
            send(snd2, zin, zsem.at[q], lax.rem(me + d, SEQ), at(q, W))

    def onward(q):
        block = cin.at[q, pl.ds(0, CHAN - 1)]
        pltpu.make_async_copy(block, block, csem.at[q]).wait()
        for t in range(W // 128):
            cols = slice(t * 128, (t + 1) * 128)
            for r in range(2):
                for p in range(CHAN):
                    sf[(r * 8 + p) * 32:(r * 8 + p + 1) * 32, :] = cin[q, p, r * 32:(r + 1) * 32, cols].astype(F32)

            def pick(s, c, t=t):
                snd2[s, :, at(q * (W // 128) + t, 128)] = sf[pl.ds(s, 16, stride=SEQ), :].astype(BF16)
                return c

            lax.fori_loop(0, SEQ, pick, 0, unroll=8)
        lanes = at(q, W)
        zin[me, :, lanes] = snd2[me, :, lanes]
        group(q, range(8))

    def gate_rows(i, c):
        g = gat[i].astype(F32)
        gp[at(i, 16), :] = jnp.concatenate([g[:, 0, :], g[:, 1, :]], axis=0).astype(BF16)
        return c

    row_of = lax.rem(lax.div(lax.broadcasted_iota(jnp.int32, (128, 128), 1), CHAN), 2)

    def project_rows(k, c):
        for p in range(CHAN):
            for r in range(2):
                sp[pl.ds(r * CHAN + p, CL, stride=2 * CHAN), :] = pr[p * CL:(p + 1) * CL, at(k, 128)].astype(F32)
        st[...] = sp[...].T
        for q in range(NQ):
            for r in range(2):
                sb[pl.ds(r, 128, stride=2), :] = jnp.where(row_of == r, st[:, q * 128:(q + 1) * 128], 0.0)
            if q < NQ - 1:
                pb[q, at(k, 256), :] = sb[...].astype(BF16)
            else:
                pb5[at(k, 256), :] = sb[...].astype(BF16)
        return c

    def stage(q, c):
        @pl.when(lax.rem(q, 2) == 0)
        def _():
            h = lax.div(q, 2)
            arrived(xin, xsem.at[h], at(h, WH))

        middle(q)

        @pl.when(q > 0)
        def _():
            onward(q - 1)

        return c

    lax.fori_loop(0, 2, stage, 0)
    lax.fori_loop(0, CL, gate_rows, 0)
    lax.fori_loop(2, 4, stage, 0)
    lax.fori_loop(0, D // 128, project_rows, 0)
    acc[...] = jnp.zeros_like(acc)
    lax.fori_loop(4, NQ, stage, 0)
    onward(NQ - 1)

    def mix(q, g):
        arrived(zin, zsem.at[q], at(q, W))

        def regroup(k, c):
            for g in range(CQ // 4):
                lanes = at(q * (CQ // 4) + g, 128)
                tiles = [zin[4 * k + j, :, lanes].astype(F32) for j in range(4)]
                outs = swap_groups(tiles, hi, odd)
                for j in range(4):
                    lb[(4 * g + j) * 16:(4 * g + j + 1) * 16, at(k, 128)] = outs[j].astype(BF16)
            return c

        lax.fori_loop(0, B // 128, regroup, 0, unroll=UNROLL)

        def columns(n, c):
            cols = at(n, 256)
            m = nt(lb[...], u1[cols, :]).astype(BF16).astype(F32)
            m = m * gp[at(q, CQ * 16), cols].astype(F32)
            g[:, cols] = m.astype(BF16)
            return c

        lax.fori_loop(0, B // 256, columns, 0, unroll=UNROLL)

    def mix_add(q, c):
        mix(q, g4)

        def add(n, c):
            cols = at(n, 256)
            acc[:, cols] += jnp.dot(pb[q], g4[:, cols], preferred_element_type=F32)
            return c

        lax.fori_loop(0, B // 256, add, 0)
        return c

    lax.fori_loop(0, NQ - 1, mix_add, 0)
    mix(NQ - 1, g5)

    for buf in (snd1, snd2):
        block = buf.at[pl.ds(0, SEQ - 1)]
        pltpu.make_async_copy(block, block, ssem.at[0]).wait()
    block = cnd.at[:, pl.ds(0, CHAN - 1)]
    pltpu.make_async_copy(block, block, ssem.at[1]).wait()


def projector(acc, pb5, g5, out_h, res, sem):
    copies = []
    for n in range(B // 256):
        cols = slice(n * 256, (n + 1) * 256)
        v = acc[:, cols] + jnp.dot(pb5[...], g5[:, cols], preferred_element_type=F32)
        res[n] = v.astype(BF16).reshape(D, 2, 256)
        copies.append(pltpu.make_async_copy(res.at[n], out_h.at[:, :, pl.ds(n * 256, 256)], sem.at[n]))
        copies[-1].start()
    for c in copies:
        c.wait()


def body(*args):
    hbm = pl.BlockSpec(memory_space=pltpu.HBM)
    whole = pl.BlockSpec(memory_space=pltpu.VMEM)
    vm = pltpu.VMEM
    dma = pltpu.SemaphoreType.DMA
    parts = pl.pallas_call(
        mixer,
        out_shape=(
            jax.ShapeDtypeStruct((2 * D, B), F32),
            jax.ShapeDtypeStruct((2 * D, 128), BF16),
            jax.ShapeDtypeStruct((128, B), BF16),
        ),
        in_specs=[hbm] * 10,
        out_specs=(whole, whole, whole),
        scratch_shapes=[
            vm((CL, AL, B), BF16), vm((CL, CHAN, 2, B), BF16), vm((CL, KL, A), BF16), vm((B, B), BF16),
            vm((AL, B), F32), vm((A, A), BF16), vm((A, A), BF16), vm((KL, A), F32), vm((B, B), BF16), vm((D, D), BF16),
            vm((SEQ, 16, CL * KL), BF16), vm((SEQ, 16, CL * KL), BF16),
            vm((NQ, CHAN, 64, W), BF16), vm((NQ, CHAN, 64, W), BF16),
            vm((SEQ, 16, CL * KL), BF16), vm((SEQ, 16, CL * KL), BF16),
            vm((NQ, A, W), BF16), vm((A, 128), F32), vm((A, A), BF16), vm((A, 128), F32),
            vm((CL * 16, B), BF16), vm((16 * CQ, B), BF16), vm((A, 128), F32), vm((2 * D, 128), F32),
            vm((128, 2 * D), F32), vm((256, 128), F32), vm((NQ - 1, 2 * D, 128), BF16), vm((128, B), BF16),
            dma((4,)), dma((NH,)), dma((15,)), dma((2,)), dma((NH,)), dma((NQ,)), dma((NQ,)),
        ],
        compiler_params=pltpu.CompilerParams(
            collective_id=0, has_side_effects=True, vmem_limit_bytes=VLIM * 1024 * 1024
        ),
    )(*[pltpu.with_memory_space_constraint(x, pltpu.HBM) for x in args])
    return pl.pallas_call(
        projector,
        out_shape=jax.ShapeDtypeStruct((D, 2, B), BF16),
        in_specs=[whole, whole, whole],
        out_specs=hbm,
        scratch_shapes=[vm((B // 256, D, 2, 256), BF16), dma((B // 256,))],
        compiler_params=pltpu.CompilerParams(vmem_limit_bytes=32 * 1024 * 1024),
    )(*parts)


VLIM = 48
UNROLL = True


def solution(mesh):
    return jax.shard_map(
        body,
        mesh=mesh,
        in_specs=(
            P("chan", "seq", None),
            P(None, ("seq", "chan"), None),
            P("chan", "seq", None),
            P(),
            P("seq", None),
            P(),
            P(),
            P("seq", None),
            P(),
            P(),
        ),
        out_specs=P(None, ("seq", "chan"), None),
        check_vma=False,
    )
```

```python
import functools

import jax
import jax.numpy as jnp
from jax import lax
from jax.experimental import pallas as pl
from jax.experimental.pallas import tpu as pltpu
from jax.sharding import PartitionSpec as P

MESH = pl.DeviceIdType.MESH
F32 = jnp.float32
BF16 = jnp.bfloat16
SEQ, CHAN = 32, 8
CL, AL, B, A, KL, D = 48, 16, 1024, 512, 32, 384
CH = 16
NH = CL // CH
WH = CH * KL
CQ = 8
NQ = CL // CQ
W = CQ * KL
FAR = [d for k in range(17) for d in sorted({16 - k, 16 + k}) if 0 < d < SEQ]

EARLY = [z * 4 + y * 2 + c for y in (0, 1) for z in range(4) for c in (0, 1)] + list(range(16, SEQ))


def nt(a, b):
    return lax.dot_general(a, b, (((1,), (1,)), ((), ())), preferred_element_type=F32)


def swap_groups(v, hi, odd):
    v0, v1, v2, v3 = v
    a0 = jnp.where(hi, pltpu.roll(v2, 64, 1), v0)
    a2 = jnp.where(hi, v2, pltpu.roll(v0, 64, 1))
    a1 = jnp.where(hi, pltpu.roll(v3, 64, 1), v1)
    a3 = jnp.where(hi, v3, pltpu.roll(v1, 64, 1))
    o0 = jnp.where(odd, pltpu.roll(a1, 32, 1), a0)
    o1 = jnp.where(odd, a1, pltpu.roll(a0, 96, 1))
    o2 = jnp.where(odd, pltpu.roll(a3, 32, 1), a2)
    o3 = jnp.where(odd, a3, pltpu.roll(a2, 96, 1))
    return o0, o1, o2, o3


def at(i, n):
    return pl.ds(pl.multiple_of(i * n, n), n)


def mixer(
    tok_h, gat_h, ker_h, f1_h, tw1_h, s2_h, v2_h, tw2_h, u1_h, pr_h,
    acc, pb5, g5,
    tok, gat, ker, f1, tw1, s2, v2, tw2, u1, pr,
    snd1, xin, cnd, cin, snd2, zin, kt_, tw2t, v2p, tw2p, gp, lb, sf, sp, st, sb, pb, g4,
    fsem, tsem, lsem, ssem, xsem, csem, zsem,
):
    me = lax.axis_index("seq")
    mc = lax.axis_index("chan")
    n0 = lax.rem(lax.div(me, 8) + 2, 4)

    def f1_load(i):
        rows = at(lax.rem(n0 + i, 4), 256)
        return pltpu.make_async_copy(f1_h.at[rows], f1.at[rows], fsem.at[i])

    def tok_load(h):
        rows = pl.ds(h * CH, CH)
        return pltpu.make_async_copy(tok_h.at[rows], tok.at[rows], tsem.at[h])

    loads = [
        pltpu.make_async_copy(src, dst, lsem.at[i])
        for i, (src, dst) in enumerate(
            [(tw1_h, tw1), (s2_h, s2), (ker_h, ker), (v2_h, v2), (tw2_h, tw2), (u1_h, u1), (pr_h, pr)]
            + [(gat_h.at[pl.ds(p * CL, CL)], gat.at[:, p]) for p in range(CHAN)]
        )
    ]
    tok_load(0).start()
    f1_load(0).start()
    loads[0].start()

    barrier = pltpu.get_barrier_semaphore()
    for d in FAR:
        pl.semaphore_signal(barrier, inc=1, device_id={"seq": lax.rem(me + d, SEQ)}, device_id_type=MESH)
    for d in range(1, CHAN):
        pl.semaphore_signal(barrier, inc=1, device_id={"chan": lax.rem(mc + d, CHAN)}, device_id_type=MESH)

    for i in range(1, 4):
        f1_load(i).start()
    for h in range(1, NH):
        tok_load(h).start()
    for c in loads[1:]:
        c.start()

    lane = lax.broadcasted_iota(jnp.int32, (16, 128), 1)
    hi = lane >= 64
    odd = lax.rem(lax.div(lane, 32), 2) == 1

    def send(src, dst, sem, p, lanes):
        pltpu.make_async_remote_copy(
            src.at[p, :, lanes], dst.at[me, :, lanes], ssem.at[0], sem,
            device_id={"seq": p}, device_id_type=MESH,
        ).start()

    def arrived(dst, sem, lanes):
        block = dst.at[pl.ds(0, SEQ - 1), :, lanes]
        pltpu.make_async_copy(block, block, sem).wait()

    loads[0].wait()
    for h in range(NH):
        tok_load(h).wait()
        lanes = pl.ds(h * WH, WH)

        def first(i, c, h=h, lanes=lanes):
            n = lax.rem(n0 + i, 4)
            if h == 0:
                f1_load(i).wait()
            rows = tok[pl.ds(h * CH, CH)].reshape(CH * AL, B)
            f = nt(rows, f1[at(n, 256), :])
            for t in range(2):
                tw = tw1[:, at(2 * n + t, 128)]
                for g in range(CH // 4):
                    tiles = [f[(4 * g + j) * 16:(4 * g + j + 1) * 16, t * 128:(t + 1) * 128] * tw for j in range(4)]
                    outs = swap_groups(tiles, hi, odd)
                    for j in range(4):
                        snd1[n * 8 + t * 4 + j, :, h * WH + g * 128:h * WH + (g + 1) * 128] = outs[j].astype(BF16)
            if h == 0:
                @pl.when(i == 0)
                def _():
                    pl.semaphore_wait(barrier, SEQ - 1 + CHAN - 1)
            for j in range(8):
                p = n * 8 + j

                @pl.when(p != me)
                def _(p=p):
                    send(snd1, xin, xsem.at[h], p, lanes)

            return c

        lax.fori_loop(0, 4, first, 0)
        xin[me, :, lanes] = snd1[me, :, lanes]

    for c in loads[1:]:
        c.wait()

    def flip(q, c):
        k = ker[pl.ds(q * CQ, CQ)].reshape(W, A)
        kt_[q] = k.T
        return c

    lax.fori_loop(0, NQ, flip, 0)
    t = tw2[...]
    tw2t[...] = jnp.concatenate([t, t, t, t], axis=0).T
    for k in range(A // 128):
        sf[...] = v2[:, k * 128:(k + 1) * 128].astype(F32)

        def order(i, c, k=k):
            v2p[at(i, SEQ), k * 128:(k + 1) * 128] = sf[pl.ds(i, SEQ, stride=16), :].astype(BF16)
            if k == 0:
                tw2p[at(i, SEQ), :] = tw2t[pl.ds(i, SEQ, stride=16), :]
            return c

        lax.fori_loop(0, 16, order, 0)

    def middle(q):
        lanes = at(q, W)
        x = xin[:, :, lanes].reshape(A, W)
        spectrum = jnp.dot(s2[...], x, preferred_element_type=F32)
        scaled = (spectrum * kt_[q].astype(F32)).astype(BF16)
        inv = jnp.dot(v2p[...], scaled, preferred_element_type=F32)
        tw = tw2p[...]
        inv = (inv * jnp.concatenate([tw] * (W // 128), axis=1)).astype(BF16)
        cnd[q] = inv.reshape(CHAN, 64, W)
        cin[q, mc] = cnd[q, mc]
        for d in (4, 1, 5, 7, 3, 2, 6):
            p = lax.rem(mc + d, CHAN)
            pltpu.make_async_remote_copy(
                cnd.at[q, p], cin.at[q, mc], ssem.at[1], csem.at[q],
                device_id={"chan": p}, device_id_type=MESH,
            ).start()

    def group(q):
        for p in EARLY:
            @pl.when(p != me)
            def _(p=p):
                send(snd2, zin, zsem.at[q], p, at(q, W))

    def onward(q):
        block = cin.at[q, pl.ds(0, CHAN - 1)]
        pltpu.make_async_copy(block, block, csem.at[q]).wait()
        for t in range(W // 128):
            cols = slice(t * 128, (t + 1) * 128)
            for r in range(2):
                for p in range(CHAN):
                    sf[(r * 8 + p) * 32:(r * 8 + p + 1) * 32, :] = cin[q, p, r * 32:(r + 1) * 32, cols].astype(F32)

            def pick(s, c, t=t):
                snd2[s, :, at(q * (W // 128) + t, 128)] = sf[pl.ds(s, 16, stride=SEQ), :].astype(BF16)
                return c

            lax.fori_loop(0, SEQ, pick, 0, unroll=8)
        lanes = at(q, W)
        zin[me, :, lanes] = snd2[me, :, lanes]
        group(q)

    def gate_rows(i, c):
        g = gat[i].astype(F32)
        gp[at(i, 16), :] = jnp.concatenate([g[:, 0, :], g[:, 1, :]], axis=0).astype(BF16)
        return c

    row_of = lax.rem(lax.div(lax.broadcasted_iota(jnp.int32, (128, 128), 1), CHAN), 2)

    def project_rows(k, c):
        for p in range(CHAN):
            for r in range(2):
                sp[pl.ds(r * CHAN + p, CL, stride=2 * CHAN), :] = pr[p * CL:(p + 1) * CL, at(k, 128)].astype(F32)
        st[...] = sp[...].T
        for q in range(NQ):
            for r in range(2):
                sb[pl.ds(r, 128, stride=2), :] = jnp.where(row_of == r, st[:, q * 128:(q + 1) * 128], 0.0)
            if q < NQ - 1:
                pb[q, at(k, 256), :] = sb[...].astype(BF16)
            else:
                pb5[at(k, 256), :] = sb[...].astype(BF16)
        return c

    def stage(q, c):
        @pl.when(lax.rem(q, 2) == 0)
        def _():
            h = lax.div(q, 2)
            arrived(xin, xsem.at[h], at(h, WH))

        middle(q)

        @pl.when(q > 0)
        def _():
            onward(q - 1)

        return c

    lax.fori_loop(0, 2, stage, 0)
    lax.fori_loop(0, CL, gate_rows, 0)
    lax.fori_loop(2, 4, stage, 0)
    lax.fori_loop(0, D // 128, project_rows, 0)
    acc[...] = jnp.zeros_like(acc)
    lax.fori_loop(4, NQ, stage, 0)
    onward(NQ - 1)

    def mix(q, g):
        arrived(zin, zsem.at[q], at(q, W))

        def regroup(k, c):
            for g in range(CQ // 4):
                lanes = at(q * (CQ // 4) + g, 128)
                tiles = [zin[4 * k + j, :, lanes].astype(F32) for j in range(4)]
                outs = swap_groups(tiles, hi, odd)
                for j in range(4):
                    lb[(4 * g + j) * 16:(4 * g + j + 1) * 16, at(k, 128)] = outs[j].astype(BF16)
            return c

        lax.fori_loop(0, B // 128, regroup, 0, unroll=UNROLL)

        def columns(n, c):
            cols = at(n, 256)
            m = nt(lb[...], u1[cols, :]).astype(BF16).astype(F32)
            m = m * gp[at(q, CQ * 16), cols].astype(F32)
            g[:, cols] = m.astype(BF16)
            return c

        lax.fori_loop(0, B // 256, columns, 0, unroll=UNROLL)

    def mix_add(q, c):
        mix(q, g4)

        def add(n, c):
            cols = at(n, 256)
            acc[:, cols] += jnp.dot(pb[q], g4[:, cols], preferred_element_type=F32)
            return c

        lax.fori_loop(0, B // 256, add, 0)
        return c

    lax.fori_loop(0, NQ - 1, mix_add, 0)
    mix(NQ - 1, g5)

    for buf in (snd1, snd2):
        block = buf.at[pl.ds(0, SEQ - 1)]
        pltpu.make_async_copy(block, block, ssem.at[0]).wait()
    block = cnd.at[:, pl.ds(0, CHAN - 1)]
    pltpu.make_async_copy(block, block, ssem.at[1]).wait()


def projector(acc, pb5, g5, out_h, res, sem):
    copies = []
    for n in range(B // 256):
        cols = slice(n * 256, (n + 1) * 256)
        v = acc[:, cols] + jnp.dot(pb5[...], g5[:, cols], preferred_element_type=F32)
        res[n] = v.astype(BF16).reshape(D, 2, 256)
        copies.append(pltpu.make_async_copy(res.at[n], out_h.at[:, :, pl.ds(n * 256, 256)], sem.at[n]))
        copies[-1].start()
    for c in copies:
        c.wait()


def body(*args):
    hbm = pl.BlockSpec(memory_space=pltpu.HBM)
    whole = pl.BlockSpec(memory_space=pltpu.VMEM)
    vm = pltpu.VMEM
    dma = pltpu.SemaphoreType.DMA
    parts = pl.pallas_call(
        mixer,
        out_shape=(
            jax.ShapeDtypeStruct((2 * D, B), F32),
            jax.ShapeDtypeStruct((2 * D, 128), BF16),
            jax.ShapeDtypeStruct((128, B), BF16),
        ),
        in_specs=[hbm] * 10,
        out_specs=(whole, whole, whole),
        scratch_shapes=[
            vm((CL, AL, B), BF16), vm((CL, CHAN, 2, B), BF16), vm((CL, KL, A), BF16), vm((B, B), BF16),
            vm((AL, B), F32), vm((A, A), BF16), vm((A, A), BF16), vm((KL, A), F32), vm((B, B), BF16), vm((D, D), BF16),
            vm((SEQ, 16, CL * KL), BF16), vm((SEQ, 16, CL * KL), BF16),
            vm((NQ, CHAN, 64, W), BF16), vm((NQ, CHAN, 64, W), BF16),
            vm((SEQ, 16, CL * KL), BF16), vm((SEQ, 16, CL * KL), BF16),
            vm((NQ, A, W), BF16), vm((A, 128), F32), vm((A, A), BF16), vm((A, 128), F32),
            vm((CL * 16, B), BF16), vm((16 * CQ, B), BF16), vm((A, 128), F32), vm((2 * D, 128), F32),
            vm((128, 2 * D), F32), vm((256, 128), F32), vm((NQ - 1, 2 * D, 128), BF16), vm((128, B), BF16),
            dma((4,)), dma((NH,)), dma((15,)), dma((2,)), dma((NH,)), dma((NQ,)), dma((NQ,)),
        ],
        compiler_params=pltpu.CompilerParams(
            collective_id=0, has_side_effects=True, vmem_limit_bytes=VLIM * 1024 * 1024
        ),
    )(*[pltpu.with_memory_space_constraint(x, pltpu.HBM) for x in args])
    return pl.pallas_call(
        projector,
        out_shape=jax.ShapeDtypeStruct((D, 2, B), BF16),
        in_specs=[whole, whole, whole],
        out_specs=hbm,
        scratch_shapes=[vm((B // 256, D, 2, 256), BF16), dma((B // 256,))],
        compiler_params=pltpu.CompilerParams(vmem_limit_bytes=32 * 1024 * 1024),
    )(*parts)


VLIM = 48
UNROLL = True


def solution(mesh):
    return jax.shard_map(
        body,
        mesh=mesh,
        in_specs=(
            P("chan", "seq", None),
            P(None, ("seq", "chan"), None),
            P("chan", "seq", None),
            P(),
            P("seq", None),
            P(),
            P(),
            P("seq", None),
            P(),
            P(),
        ),
        out_specs=P(None, ("seq", "chan"), None),
        check_vma=False,
    )
```

```python
import functools

import jax
import jax.numpy as jnp
from jax import lax
from jax.experimental import pallas as pl
from jax.experimental.pallas import tpu as pltpu
from jax.sharding import PartitionSpec as P

MESH = pl.DeviceIdType.MESH
F32 = jnp.float32
BF16 = jnp.bfloat16
SEQ, CHAN = 32, 8
CL, AL, B, A, KL, D = 48, 16, 1024, 512, 32, 384
CH = 16
NH = CL // CH
WH = CH * KL
CQ = 8
NQ = CL // CQ
W = CQ * KL
FAR = [d for k in range(17) for d in sorted({16 - k, 16 + k}) if 0 < d < SEQ]

EARLY = [z * 4 + y * 2 + c for y in (0, 1) for z in range(4) for c in (0, 1)] + list(range(16, SEQ))


def nt(a, b):
    return lax.dot_general(a, b, (((1,), (1,)), ((), ())), preferred_element_type=F32)


def swap_groups(v, hi, odd):
    v0, v1, v2, v3 = v
    a0 = jnp.where(hi, pltpu.roll(v2, 64, 1), v0)
    a2 = jnp.where(hi, v2, pltpu.roll(v0, 64, 1))
    a1 = jnp.where(hi, pltpu.roll(v3, 64, 1), v1)
    a3 = jnp.where(hi, v3, pltpu.roll(v1, 64, 1))
    o0 = jnp.where(odd, pltpu.roll(a1, 32, 1), a0)
    o1 = jnp.where(odd, a1, pltpu.roll(a0, 96, 1))
    o2 = jnp.where(odd, pltpu.roll(a3, 32, 1), a2)
    o3 = jnp.where(odd, a3, pltpu.roll(a2, 96, 1))
    return o0, o1, o2, o3


def at(i, n):
    return pl.ds(pl.multiple_of(i * n, n), n)


def mixer(
    tok_h, gat_h, ker_h, f1_h, tw1_h, s2_h, v2_h, tw2_h, u1_h, pr_h,
    acc, pb5, g5,
    tok, gat, ker, f1, tw1, s2, v2, tw2, u1, pr,
    snd1, xin, cnd, cin, snd2, zin, kt_, tw2t, v2p, tw2p, gp, lb, sf, sp, st, sb, pb, g4,
    fsem, tsem, lsem, ssem, xsem, csem, zsem,
):
    me = lax.axis_index("seq")
    mc = lax.axis_index("chan")
    n0 = lax.rem(lax.div(me, 8) + 2, 4)

    def f1_load(i):
        rows = at(lax.rem(n0 + i, 4), 256)
        return pltpu.make_async_copy(f1_h.at[rows], f1.at[rows], fsem.at[i])

    def tok_load(h):
        rows = pl.ds(h * CH, CH)
        return pltpu.make_async_copy(tok_h.at[rows], tok.at[rows], tsem.at[h])

    loads = [
        pltpu.make_async_copy(src, dst, lsem.at[i])
        for i, (src, dst) in enumerate(
            [(tw1_h, tw1), (s2_h, s2), (ker_h, ker), (v2_h, v2), (tw2_h, tw2), (u1_h, u1), (pr_h, pr)]
            + [(gat_h.at[pl.ds(p * CL, CL)], gat.at[:, p]) for p in range(CHAN)]
        )
    ]
    tok_load(0).start()
    f1_load(0).start()
    loads[0].start()

    barrier = pltpu.get_barrier_semaphore()
    for d in FAR:
        pl.semaphore_signal(barrier, inc=1, device_id={"seq": lax.rem(me + d, SEQ)}, device_id_type=MESH)
    for d in range(1, CHAN):
        pl.semaphore_signal(barrier, inc=1, device_id={"chan": lax.rem(mc + d, CHAN)}, device_id_type=MESH)

    for i in range(1, 4):
        f1_load(i).start()
    for h in range(1, NH):
        tok_load(h).start()
    for c in loads[1:]:
        c.start()

    lane = lax.broadcasted_iota(jnp.int32, (16, 128), 1)
    hi = lane >= 64
    odd = lax.rem(lax.div(lane, 32), 2) == 1

    def send(src, dst, sem, p, lanes):
        pltpu.make_async_remote_copy(
            src.at[p, :, lanes], dst.at[me, :, lanes], ssem.at[0], sem,
            device_id={"seq": p}, device_id_type=MESH,
        ).start()

    def arrived(dst, sem, lanes):
        block = dst.at[pl.ds(0, SEQ - 1), :, lanes]
        pltpu.make_async_copy(block, block, sem).wait()

    loads[0].wait()
    for h in range(NH):
        tok_load(h).wait()
        lanes = pl.ds(h * WH, WH)

        def first(i, c, h=h, lanes=lanes):
            n = lax.rem(n0 + i, 4)
            if h == 0:
                f1_load(i).wait()
            rows = tok[pl.ds(h * CH, CH)].reshape(CH * AL, B)
            f = nt(rows, f1[at(n, 256), :])
            for t in range(2):
                tw = tw1[:, at(2 * n + t, 128)]
                for g in range(CH // 4):
                    tiles = [f[(4 * g + j) * 16:(4 * g + j + 1) * 16, t * 128:(t + 1) * 128] * tw for j in range(4)]
                    outs = swap_groups(tiles, hi, odd)
                    for j in range(4):
                        snd1[n * 8 + t * 4 + j, :, h * WH + g * 128:h * WH + (g + 1) * 128] = outs[j].astype(BF16)
            if h == 0:
                @pl.when(i == 0)
                def _():
                    pl.semaphore_wait(barrier, SEQ - 1 + CHAN - 1)
            for j in range(8):
                p = n * 8 + j

                @pl.when(p != me)
                def _(p=p):
                    send(snd1, xin, xsem.at[h], p, lanes)

            return c

        lax.fori_loop(0, 4, first, 0)
        xin[me, :, lanes] = snd1[me, :, lanes]

    for c in loads[1:]:
        c.wait()

    def flip(q, c):
        k = ker[pl.ds(q * CQ, CQ)].reshape(W, A)
        kt_[q] = k.T
        return c

    lax.fori_loop(0, NQ, flip, 0)
    t = tw2[...]
    tw2t[...] = jnp.concatenate([t, t, t, t], axis=0).T
    for k in range(A // 128):
        sf[...] = v2[:, k * 128:(k + 1) * 128].astype(F32)

        def order(i, c, k=k):
            v2p[at(i, SEQ), k * 128:(k + 1) * 128] = sf[pl.ds(i, SEQ, stride=16), :].astype(BF16)
            if k == 0:
                tw2p[at(i, SEQ), :] = tw2t[pl.ds(i, SEQ, stride=16), :]
            return c

        lax.fori_loop(0, 16, order, 0)

    def middle(q):
        lanes = at(q, W)
        x = xin[:, :, lanes].reshape(A, W)
        spectrum = jnp.dot(s2[...], x, preferred_element_type=F32)
        scaled = (spectrum * kt_[q].astype(F32)).astype(BF16)
        inv = jnp.dot(v2p[...], scaled, preferred_element_type=F32)
        tw = tw2p[...]
        inv = (inv * jnp.concatenate([tw] * (W // 128), axis=1)).astype(BF16)
        cnd[q] = inv.reshape(CHAN, 64, W)
        cin[q, mc] = cnd[q, mc]
        for d in (4, 1, 5, 7, 3, 2, 6):
            p = lax.rem(mc + d, CHAN)
            pltpu.make_async_remote_copy(
                cnd.at[q, p], cin.at[q, mc], ssem.at[1], csem.at[q],
                device_id={"chan": p}, device_id_type=MESH,
            ).start()

    def group(q):
        for p in EARLY:
            @pl.when(p != me)
            def _(p=p):
                send(snd2, zin, zsem.at[q], p, at(q, W))

    def onward(q):
        block = cin.at[q, pl.ds(0, CHAN - 1)]
        pltpu.make_async_copy(block, block, csem.at[q]).wait()
        for t in range(W // 128):
            cols = slice(t * 128, (t + 1) * 128)
            for r in range(2):
                for p in range(CHAN):
                    sf[(r * 8 + p) * 32:(r * 8 + p + 1) * 32, :] = cin[q, p, r * 32:(r + 1) * 32, cols].astype(F32)

            def pick(s, c, t=t):
                snd2[s, :, at(q * (W // 128) + t, 128)] = sf[pl.ds(s, 16, stride=SEQ), :].astype(BF16)
                return c

            lax.fori_loop(0, SEQ, pick, 0, unroll=8)
        lanes = at(q, W)
        zin[me, :, lanes] = snd2[me, :, lanes]
        group(q)

    def gate_rows(i, c):
        g = gat[i].astype(F32)
        gp[at(i, 16), :] = jnp.concatenate([g[:, 0, :], g[:, 1, :]], axis=0).astype(BF16)
        return c

    row_of = lax.rem(lax.div(lax.broadcasted_iota(jnp.int32, (128, 128), 1), CHAN), 2)

    def project_rows(k, c):
        for p in range(CHAN):
            for r in range(2):
                sp[pl.ds(r * CHAN + p, CL, stride=2 * CHAN), :] = pr[p * CL:(p + 1) * CL, at(k, 128)].astype(F32)
        st[...] = sp[...].T
        for q in range(NQ):
            for r in range(2):
                sb[pl.ds(r, 128, stride=2), :] = jnp.where(row_of == r, st[:, q * 128:(q + 1) * 128], 0.0)
            if q < NQ - 1:
                pb[q, at(k, 256), :] = sb[...].astype(BF16)
            else:
                pb5[at(k, 256), :] = sb[...].astype(BF16)
        return c

    def stage(q, c):
        @pl.when(lax.rem(q, 2) == 0)
        def _():
            h = lax.div(q, 2)
            arrived(xin, xsem.at[h], at(h, WH))

        middle(q)

        @pl.when(q > 0)
        def _():
            onward(q - 1)

        return c

    lax.fori_loop(0, 2, stage, 0)
    lax.fori_loop(0, CL, gate_rows, 0)
    lax.fori_loop(2, 4, stage, 0)
    lax.fori_loop(0, D // 128, project_rows, 0)
    acc[...] = jnp.zeros_like(acc)
    lax.fori_loop(4, NQ, stage, 0)
    onward(NQ - 1)

    def mix(q, g):
        arrived(zin, zsem.at[q], at(q, W))

        def regroup(k, c):
            for g in range(CQ // 4):
                lanes = at(q * (CQ // 4) + g, 128)
                tiles = [zin[4 * k + j, :, lanes].astype(F32) for j in range(4)]
                outs = swap_groups(tiles, hi, odd)
                for j in range(4):
                    lb[(4 * g + j) * 16:(4 * g + j + 1) * 16, at(k, 128)] = outs[j].astype(BF16)
            return c

        lax.fori_loop(0, B // 128, regroup, 0, unroll=UNROLL)

        def columns(n, c):
            cols = at(n, 256)
            m = nt(lb[...], u1[cols, :]).astype(BF16).astype(F32)
            m = m * gp[at(q, CQ * 16), cols].astype(F32)
            g[:, cols] = m.astype(BF16)
            return c

        lax.fori_loop(0, B // 256, columns, 0, unroll=UNROLL)

    def mix_add(q, c):
        mix(q, g4)

        def add(n, c):
            cols = at(n, 256)
            acc[:, cols] += jnp.dot(pb[q], g4[:, cols], preferred_element_type=F32)
            return c

        lax.fori_loop(0, B // 256, add, 0)
        return c

    lax.fori_loop(0, NQ - 1, mix_add, 0)
    mix(NQ - 1, g5)

    for buf in (snd1, snd2):
        block = buf.at[pl.ds(0, SEQ - 1)]
        pltpu.make_async_copy(block, block, ssem.at[0]).wait()
    block = cnd.at[:, pl.ds(0, CHAN - 1)]
    pltpu.make_async_copy(block, block, ssem.at[1]).wait()


def projector(acc, pb5, g5, out_h, res, sem):
    copies = []
    for n in range(B // PIECE):
        cols = slice(n * PIECE, (n + 1) * PIECE)
        v = acc[:, cols] + jnp.dot(pb5[...], g5[:, cols], preferred_element_type=F32)
        res[n] = v.astype(BF16).reshape(D, 2, PIECE)
        copies.append(pltpu.make_async_copy(res.at[n], out_h.at[:, :, pl.ds(n * PIECE, PIECE)], sem.at[n]))
        copies[-1].start()
    for c in copies:
        c.wait()


def body(*args):
    hbm = pl.BlockSpec(memory_space=pltpu.HBM)
    whole = pl.BlockSpec(memory_space=pltpu.VMEM)
    vm = pltpu.VMEM
    dma = pltpu.SemaphoreType.DMA
    parts = pl.pallas_call(
        mixer,
        out_shape=(
            jax.ShapeDtypeStruct((2 * D, B), F32),
            jax.ShapeDtypeStruct((2 * D, 128), BF16),
            jax.ShapeDtypeStruct((128, B), BF16),
        ),
        in_specs=[hbm] * 10,
        out_specs=(whole, whole, whole),
        scratch_shapes=[
            vm((CL, AL, B), BF16), vm((CL, CHAN, 2, B), BF16), vm((CL, KL, A), BF16), vm((B, B), BF16),
            vm((AL, B), F32), vm((A, A), BF16), vm((A, A), BF16), vm((KL, A), F32), vm((B, B), BF16), vm((D, D), BF16),
            vm((SEQ, 16, CL * KL), BF16), vm((SEQ, 16, CL * KL), BF16),
            vm((NQ, CHAN, 64, W), BF16), vm((NQ, CHAN, 64, W), BF16),
            vm((SEQ, 16, CL * KL), BF16), vm((SEQ, 16, CL * KL), BF16),
            vm((NQ, A, W), BF16), vm((A, 128), F32), vm((A, A), BF16), vm((A, 128), F32),
            vm((CL * 16, B), BF16), vm((16 * CQ, B), BF16), vm((A, 128), F32), vm((2 * D, 128), F32),
            vm((128, 2 * D), F32), vm((256, 128), F32), vm((NQ - 1, 2 * D, 128), BF16), vm((128, B), BF16),
            dma((4,)), dma((NH,)), dma((15,)), dma((2,)), dma((NH,)), dma((NQ,)), dma((NQ,)),
        ],
        compiler_params=pltpu.CompilerParams(
            collective_id=0, has_side_effects=True, vmem_limit_bytes=VLIM * 1024 * 1024
        ),
    )(*[pltpu.with_memory_space_constraint(x, pltpu.HBM) for x in args])
    return pl.pallas_call(
        projector,
        out_shape=jax.ShapeDtypeStruct((D, 2, B), BF16),
        in_specs=[whole, whole, whole],
        out_specs=hbm,
        scratch_shapes=[vm((B // PIECE, D, 2, PIECE), BF16), dma((B // PIECE,))],
        compiler_params=pltpu.CompilerParams(vmem_limit_bytes=32 * 1024 * 1024),
    )(*parts)


VLIM = 48
UNROLL = True
PIECE = 512


def solution(mesh):
    return jax.shard_map(
        body,
        mesh=mesh,
        in_specs=(
            P("chan", "seq", None),
            P(None, ("seq", "chan"), None),
            P("chan", "seq", None),
            P(),
            P("seq", None),
            P(),
            P(),
            P("seq", None),
            P(),
            P(),
        ),
        out_specs=P(None, ("seq", "chan"), None),
        check_vma=False,
    )
```
